32 devices in a mesh: frame: 16 (over z, y, core), rec: 2 (over x).
Axes of the slice: x: 2, y: 2, z: 4, core: 2. Of those that a mesh axis runs over, the one named last changes fastest.
Arguments:
- code_indices: int32 [2, 4096, 8], P('rec', 'frame'), may hold values from 0 to 7
- lengths: int32 [2], P('rec'), may hold values from 2048 to 4096
- cotangent: bfloat16 [2, 1310720], P('rec', 'frame'), may hold values from -6 to 6
- embed_weight: float32 [8, 512], replicated, may hold values from -2 to 2
- embed_bias: float32 [512], replicated, may hold values from -3 to 3
- depth_kernel: float32 [7, 512], replicated, may hold values from -2 to 2
- depth_bias: float32 [512], replicated, may hold values from -3 to 3
- norm_gain: float32 [512], replicated, may hold values from 0.5 to 1.5
- norm_bias: float32 [512], replicated, may hold values from -1.75 to 1.75
- up_weight: bfloat16 [512, 1536], replicated, may hold values from -0.25 to 0.25
- up_bias: float32 [1536], replicated, may hold values from -3 to 3
- down_weight: bfloat16 [1536, 512], replicated, may hold values from -0.15625 to 0.15625
- down_bias: float32 [512], replicated, may hold values from -1.75 to 1.75
- layer_scale: float32 [512], replicated, may hold values from 0.3 to 1
- head_weight: bfloat16 [512, 1280], replicated, may hold values from -0.25 to 0.25
- head_bias: float32 [1280], replicated, may hold values from -3 to 3
Outputs:
- embed_weight_grad: float32 [8, 512], P(None, 'frame')
- embed_bias_grad: float32 [512], P('frame')
- depth_kernel_grad: float32 [7, 512], P(None, 'frame')
- depth_bias_grad: float32 [512], P('frame')
- norm_gain_grad: float32 [512], P('frame')
- norm_bias_grad: float32 [512], P('frame')
- up_weight_grad: float32 [512, 1536], P('frame')
- up_bias_grad: float32 [1536], P('frame')
- down_weight_grad: float32 [1536, 512], P('frame')
- down_bias_grad: float32 [512], P('frame')
- layer_scale_grad: float32 [512], P('frame')
- head_weight_grad: float32 [512, 1280], P('frame')
- head_bias_grad: float32 [1280], P('frame')
The draws below stay inside these ranges and needn't reach their ends.
Inputs may be any that keep to these rules, and one draw needn't show every extreme that they name: `lengths`: frames at or after a recording's length are padding.
All inputs are finite; a program needn't handle non-finite values.
Results may differ from the reference program's by a relative error of at most 0.011.
Values may be sent and summed in bfloat16 or wider, within the bound.
A program may use at most 64 MiB of HBM per device.

```python
import jax
import jax.numpy as jnp
from jax import lax

D = 512
FF = 1536
Q = 8
LEVELS = 8
KERNEL = 7
NFFT = 1280
HOP = 320
BINS = 640
PAD = 480
FRAMES = 4096
RECS = 2
SAMPLES = 1310720


def plant(values, key, least, high):
    spot = [jax.random.randint(jax.random.fold_in(key, axis), (), 0, length) for axis, length in enumerate(values.shape)]
    widest = values.shape.index(max(values.shape))
    neighbour = spot[:widest] + [(spot[widest] + 1) % values.shape[widest]] + spot[widest + 1:]
    return values.at[tuple(spot)].set(least).at[tuple(neighbour)].set(high)


def steps_of(key, extent, shards, smallest, largest):
    factor_of, own = 1.0, jax.random.fold_in(key, 6)
    for dim, shards_of in shards:
        draws = jnp.exp(jax.random.uniform(jax.random.fold_in(own, dim), (shards_of,), jnp.float32, smallest / len(shards), largest / len(shards)))
        factor_of = factor_of * jnp.repeat(draws, extent[dim] // shards_of).reshape([-1 if axis == dim else 1 for axis in range(len(extent))])
    return factor_of


def bell_draw(rng, shape, deviation, bound, shards=(), held_as=jnp.bfloat16):
    result = deviation * jax.random.normal(rng, shape, jnp.float32)
    if shards:
        result = result * steps_of(rng, shape, shards, -0.22, 0.18)
    return jnp.clip(result, -bound, bound).astype(held_as)


def setup_inputs(seed: int = 0) -> dict:
    streams_of = jax.random.split(jax.random.key(seed), 17)
    code_indices = plant(jax.random.randint(streams_of[0], (RECS, FRAMES, Q), 0, LEVELS), jax.random.fold_in(streams_of[0], 1), 0, LEVELS - 1).astype(jnp.int32)
    lengths = jax.random.randint(streams_of[1], (RECS,), FRAMES // 2, FRAMES + 1).astype(jnp.int32)
    cotangent = bell_draw(streams_of[2], (RECS, SAMPLES), 1.0, 6.0, ((0, 2), (1, 16)))
    embed_weight = bell_draw(streams_of[3], (Q, D), Q ** -0.5, 2.0, (), jnp.float32)
    embed_bias = bell_draw(streams_of[4], (D,), 0.5, 3.0, (), jnp.float32)
    depth_kernel = bell_draw(streams_of[5], (KERNEL, D), KERNEL ** -0.5, 2.0, (), jnp.float32)
    depth_bias = bell_draw(streams_of[6], (D,), 0.5, 3.0, (), jnp.float32)
    norm_gain = jnp.clip(1.0 + 0.1 * jax.random.normal(streams_of[7], (D,), jnp.float32), 0.5, 1.5)
    norm_bias = bell_draw(streams_of[8], (D,), 0.3, 1.75, (), jnp.float32)
    up_weight = bell_draw(streams_of[9], (D, FF), D ** -0.5, 0.25)
    up_bias = bell_draw(streams_of[10], (FF,), 0.5, 3.0, (), jnp.float32)
    down_weight = bell_draw(streams_of[11], (FF, D), FF ** -0.5, 0.15625)
    down_bias = bell_draw(streams_of[12], (D,), 0.3, 1.75, (), jnp.float32)
    layer_scale = jnp.clip(jax.random.uniform(streams_of[13], (D,), jnp.float32, 0.3, 1.0), 0.3, 1.0)
    head_weight = bell_draw(streams_of[14], (D, 2 * BINS), D ** -0.5, 0.25)
    head_bias = bell_draw(streams_of[15], (2 * BINS,), 0.5, 3.0, (), jnp.float32)
    return dict(code_indices=code_indices, lengths=lengths, cotangent=cotangent, embed_weight=embed_weight, embed_bias=embed_bias, depth_kernel=depth_kernel, depth_bias=depth_bias, norm_gain=norm_gain, norm_bias=norm_bias, up_weight=up_weight, up_bias=up_bias, down_weight=down_weight, down_bias=down_bias, layer_scale=layer_scale, head_weight=head_weight, head_bias=head_bias)


EPSILON = 1e-06

def hann_square(position, fft_size):
    window = 0.5 - 0.5 * jnp.cos(2.0 * jnp.pi / fft_size * position)
    return window * window

def synthesis(fft_size, bin_count):
    sample = jnp.arange(fft_size, dtype=jnp.int32)[:, None]
    frequency = jnp.arange(bin_count, dtype=jnp.int32)[None, :]
    turn_count = (sample * frequency % fft_size).astype(jnp.float32)
    angles = 2.0 * jnp.pi / fft_size * turn_count
    window = 0.5 - 0.5 * jnp.cos(2.0 * jnp.pi / fft_size * sample.astype(jnp.float32))
    factor = jnp.where(frequency == 0, 1.0, 2.0).astype(jnp.float32) * window / fft_size
    real_part = factor * jnp.cos(angles)
    imag_part = jnp.where(frequency == 0, 0.0, -factor * jnp.sin(angles))
    return jnp.concatenate([real_part, imag_part], axis=1).astype(jnp.bfloat16)

def sample_scale(first_sample, sample_count, total_frames, hop_size, fft_size, length):
    pad_size = (fft_size - hop_size) // 2
    sample = first_sample + jnp.arange(sample_count, dtype=jnp.int32)
    block_id = sample // hop_size
    offset = sample - block_id * hop_size + pad_size
    envelope = jnp.zeros((sample_count,), jnp.float32)
    for step_back in range(-2, 3):
        frame_id = block_id - step_back
        inside = offset + step_back * hop_size
        usable = (frame_id >= 0) & (frame_id < total_frames) & (inside >= 0) & (inside < fft_size)
        square = hann_square(inside.astype(jnp.float32), fft_size)
        envelope = envelope + jnp.where(usable, square, 0.0)
    alive_mask = sample < length * hop_size
    return jnp.where(alive_mask, 1.0 / envelope, 0.0)

def layer_norm(conv_out, norm_gain, norm_bias):
    centre = conv_out - lax.optimization_barrier(jnp.mean(conv_out, axis=-1, keepdims=True))
    spread = lax.optimization_barrier(jnp.mean(centre * centre, axis=-1, keepdims=True))
    return centre * lax.rsqrt(spread + EPSILON) * norm_gain + norm_bias

def exact_gelu(hidden_pre):
    return jax.nn.gelu(hidden_pre, approximate=False)

def head_map(logits):
    bin_count = logits.shape[1] // 2
    magnitude = jnp.exp(logits[:, :bin_count])
    phase_angle = logits[:, bin_count:]
    return jnp.concatenate([magnitude * jnp.cos(phase_angle), magnitude * jnp.sin(phase_angle)], axis=1)

def contract_rows(former, latter, precision=None):
    return lax.dot_general(former, latter, (((0,), (0,)), ((), ())), precision=precision, preferred_element_type=jnp.float32)

def contract_cols(former, latter):
    return lax.dot_general(former, latter, (((1,), (1,)), ((), ())), preferred_element_type=jnp.float32)

def recording_grads(code_rows, length, cot_row, table, embed_weight, embed_bias, depth_kernel, depth_bias, norm_gain, norm_bias, up_weight, up_bias, down_weight, down_bias, layer_scale, head_weight, head_bias):
    frame_count = code_rows.shape[0]
    frame_ids = jnp.arange(frame_count, dtype=jnp.int32)
    valid = (frame_ids < length).astype(jnp.float32)
    levels_half = (LEVELS - 1) / 2.0
    values = (code_rows.astype(jnp.float32) - levels_half) / levels_half
    projected = jnp.dot(values, embed_weight, precision=lax.Precision.HIGHEST) + embed_bias
    features = (valid[:, None] * projected).astype(jnp.bfloat16)
    padded = jnp.pad(features, ((3, 3), (0, 0)))
    conv_out = jnp.zeros((frame_count, features.shape[1]), jnp.float32) + depth_bias
    for tap_index in range(KERNEL):
        conv_out = conv_out + depth_kernel[tap_index] * padded[tap_index:tap_index + frame_count].astype(jnp.float32)
    normed, norm_pullback = jax.vjp(layer_norm, conv_out, norm_gain, norm_bias)
    normed_low = normed.astype(jnp.bfloat16)
    hidden_pre = jnp.dot(normed_low, up_weight, preferred_element_type=jnp.float32) + up_bias
    activated, gelu_pullback = jax.vjp(exact_gelu, hidden_pre)
    activated_low = activated.astype(jnp.bfloat16)
    branch = jnp.dot(activated_low, down_weight, preferred_element_type=jnp.float32) + down_bias
    latent = (features.astype(jnp.float32) + layer_scale * branch).astype(jnp.bfloat16)
    logits = jnp.dot(latent, head_weight, preferred_element_type=jnp.float32) + head_bias
    spectrum, head_pullback = jax.vjp(head_map, logits)
    sample_weight = sample_scale(0, frame_count * HOP, frame_count, HOP, NFFT, length)
    sample_grad = (cot_row.astype(jnp.float32) * sample_weight).astype(jnp.bfloat16)
    extended = jnp.pad(sample_grad, (PAD, PAD))
    hop_rows = extended.reshape(frame_count + 3, HOP)
    frame_grad = jnp.concatenate([hop_rows[quarter:quarter + frame_count] for quarter in range(4)], axis=1)
    spec_grad = jnp.dot(frame_grad, table, preferred_element_type=jnp.float32)
    logit_grad = head_pullback(spec_grad)[0]
    logit_low = logit_grad.astype(jnp.bfloat16)
    head_weight_grad = contract_rows(latent, logit_low)
    head_bias_grad = lax.optimization_barrier(jnp.sum(logit_grad, axis=0))
    latent_grad = contract_cols(logit_low, head_weight)
    layer_scale_grad = lax.optimization_barrier(jnp.sum(latent_grad * branch, axis=0))
    branch_grad = layer_scale * latent_grad
    down_bias_grad = lax.optimization_barrier(jnp.sum(branch_grad, axis=0))
    branch_low = branch_grad.astype(jnp.bfloat16)
    down_weight_grad = contract_rows(activated_low, branch_low)
    activated_grad = contract_cols(branch_low, down_weight)
    hidden_grad = gelu_pullback(activated_grad)[0]
    up_bias_grad = lax.optimization_barrier(jnp.sum(hidden_grad, axis=0))
    hidden_low = hidden_grad.astype(jnp.bfloat16)
    up_weight_grad = contract_rows(normed_low, hidden_low)
    normed_grad = contract_cols(hidden_low, up_weight)
    conv_grad, norm_gain_grad, norm_bias_grad = norm_pullback(normed_grad)
    depth_kernel_grad = jnp.stack([lax.optimization_barrier(jnp.sum(conv_grad * padded[tap_index:tap_index + frame_count].astype(jnp.float32), axis=0)) for tap_index in range(KERNEL)], axis=0)
    depth_bias_grad = lax.optimization_barrier(jnp.sum(conv_grad, axis=0))
    conv_rims = jnp.pad(conv_grad, ((3, 3), (0, 0)))
    feature_grad = latent_grad
    for tap_index in range(KERNEL):
        feature_grad = feature_grad + depth_kernel[tap_index] * conv_rims[6 - tap_index:6 - tap_index + frame_count]
    feature_grad = valid[:, None] * feature_grad
    embed_weight_grad = contract_rows(values, feature_grad, lax.Precision.HIGHEST)
    embed_bias_grad = lax.optimization_barrier(jnp.sum(feature_grad, axis=0))
    return (embed_weight_grad, embed_bias_grad, depth_kernel_grad, depth_bias_grad, norm_gain_grad, norm_bias_grad, up_weight_grad, up_bias_grad, down_weight_grad, down_bias_grad, layer_scale_grad, head_weight_grad, head_bias_grad)

def reference(code_indices, lengths, cotangent, embed_weight, embed_bias, depth_kernel, depth_bias, norm_gain, norm_bias, up_weight, up_bias, down_weight, down_bias, layer_scale, head_weight, head_bias):
    table = synthesis(NFFT, BINS)
    totals = None
    for record_index in range(RECS):
        grads = recording_grads(code_indices[record_index], lengths[record_index], cotangent[record_index], table, embed_weight, embed_bias, depth_kernel, depth_bias, norm_gain, norm_bias, up_weight, up_bias, down_weight, down_bias, layer_scale, head_weight, head_bias)
        totals = grads if totals is None else tuple((former + latter for former, latter in zip(totals, grads)))
    return (totals[0], totals[1], totals[2], totals[3], totals[4], totals[5], totals[6], totals[7], totals[8], totals[9], totals[10], totals[11], totals[12])
```

```python
import jax
import jax.numpy as jnp
from jax import lax
from jax.experimental import pallas as pl
from jax.experimental.pallas import tpu as pltpu
from jax.sharding import PartitionSpec as P

LEVELS = 8
KERNEL = 7
NFFT = 1280
HOP = 320
BINS = 640
PAD = 480


EPSILON = 1e-06


def padded_2(block, sides, width):
    for axis, dim in sides:
        count = lax.axis_size(axis)
        forward = [(i, i + 1) for i in range(count - 1)]
        backward = [(target, source) for source, target in forward]
        low = lax.ppermute(
            lax.slice_in_dim(block, block.shape[dim] - width, None, axis=dim), axis, forward
        )
        high = lax.ppermute(lax.slice_in_dim(block, 0, width, axis=dim), axis, backward)
        block = jnp.concatenate([low, block, high], axis=dim)
    return block


def hann_square(position, fft_size):
    window = 0.5 - 0.5 * jnp.cos(2.0 * jnp.pi / fft_size * position)
    return window * window


def synthesis(fft_size, bin_count):
    fine_count = 40
    frequency = jnp.arange(bin_count, dtype=jnp.int32)[None, :]

    def turns(sample):
        angle = (2.0 * jnp.pi / fft_size) * (sample * frequency % fft_size).astype(jnp.float32)
        return lax.optimization_barrier((jnp.cos(angle), jnp.sin(angle)))

    coarse_cos, coarse_sin = turns(
        jnp.arange(0, fft_size, fine_count, dtype=jnp.int32)[:, None]
    )
    fine_cos, fine_sin = turns(jnp.arange(fine_count, dtype=jnp.int32)[:, None])
    sample = jnp.arange(fft_size, dtype=jnp.float32)
    window = lax.optimization_barrier(
        (0.5 - 0.5 * jnp.cos(2.0 * jnp.pi / fft_size * sample)) / fft_size
    ).reshape(fft_size // fine_count, fine_count, 1)
    factor = window * jnp.where(frequency == 0, 1.0, 2.0)[None]
    cc, cs = coarse_cos[:, None, :], coarse_sin[:, None, :]
    fc, fs = fine_cos[None], fine_sin[None]
    real_part = factor * (cc * fc - cs * fs)
    imag_part = jnp.where(frequency[None] == 0, 0.0, -factor * (cs * fc + cc * fs))
    shape = (fft_size, bin_count)
    return (
        real_part.astype(jnp.bfloat16).reshape(shape),
        imag_part.astype(jnp.bfloat16).reshape(shape),
    )


def sample_scale(first_sample, sample_count, total_frames, hop_size, fft_size, length):
    pad_size = (fft_size - hop_size) // 2
    sample = first_sample + jnp.arange(sample_count, dtype=jnp.int32)
    block_id = sample // hop_size
    offset = sample - block_id * hop_size + pad_size
    envelope = jnp.zeros((sample_count,), jnp.float32)
    for step_back in range(-2, 3):
        frame_id = block_id - step_back
        inside = offset + step_back * hop_size
        usable = (frame_id >= 0) & (frame_id < total_frames) & (inside >= 0) & (inside < fft_size)
        square = hann_square(inside.astype(jnp.float32), fft_size)
        envelope = envelope + jnp.where(usable, square, 0.0)
    alive_mask = sample < length * hop_size
    return jnp.where(alive_mask, 1.0 / envelope, 0.0)


def layer_norm(conv_out, norm_gain, norm_bias):
    centre = conv_out - jnp.mean(conv_out, axis=-1, keepdims=True)
    spread = jnp.mean(centre * centre, axis=-1, keepdims=True)
    return centre * lax.rsqrt(spread + EPSILON) * norm_gain + norm_bias


def exact_gelu(hidden_pre):
    return jax.nn.gelu(hidden_pre, approximate=False)


def head_map(logits):
    bin_count = logits.shape[1] // 2
    magnitude = jnp.exp(logits[:, :bin_count])
    phase_angle = logits[:, bin_count:]
    return jnp.concatenate(
        [magnitude * jnp.cos(phase_angle), magnitude * jnp.sin(phase_angle)], axis=1
    )


def contract_rows(former, latter, precision=None):
    return lax.dot_general(
        former,
        latter,
        (((0,), (0,)), ((), ())),
        precision=precision,
        preferred_element_type=jnp.float32,
    )


def contract_cols(former, latter):
    return lax.dot_general(
        former, latter, (((1,), (1,)), ((), ())), preferred_element_type=jnp.float32
    )


def embed_rows(code_rows, valid_rows, embed_weight, embed_bias):
    levels_half = (LEVELS - 1) / 2.0
    values = (code_rows.astype(jnp.float32) - levels_half) / levels_half
    projected = jnp.dot(values, embed_weight, precision=lax.Precision.HIGHEST) + embed_bias
    return (values, (valid_rows[:, None] * projected).astype(jnp.bfloat16))


def reduce_kernel(chips, recs, arrays, *refs):
    groups = [refs[i * arrays : (i + 1) * arrays] for i in range(7)]
    ins, outs, pair_in, pair_sum, chip_in, final, final_in = groups
    pair_send, pair_recv, chip_send, chip_recv, rec_send, rec_recv = refs[7 * arrays :]
    total = chips * recs
    frame, rec = lax.axis_index("frame"), lax.axis_index("rec")
    core = lax.rem(frame, 2)
    chip = lax.div(frame, 2)
    me = rec * chips + chip
    partner = frame + 1 - 2 * core

    def place(step):
        target = lax.rem(me + step, total)
        return lax.rem(target, chips), lax.div(target, chips)

    def pair_copy(i, step):
        j, h = place(step)
        return pltpu.make_async_remote_copy(
            src_ref=ins[i].at[j, 1 - core, h],
            dst_ref=pair_in[i].at[j, h],
            send_sem=pair_send.at[i, step],
            recv_sem=pair_recv.at[i, step],
            device_id={"rec": rec, "frame": partner},
            device_id_type=pl.DeviceIdType.MESH,
        )

    def chip_copy(i, step):
        j, h = place(step)
        return pltpu.make_async_remote_copy(
            src_ref=pair_sum[i].at[j, h],
            dst_ref=chip_in[i].at[step],
            send_sem=chip_send.at[i, step],
            recv_sem=chip_recv.at[i, step],
            device_id={"rec": h, "frame": 2 * j + core},
            device_id_type=pl.DeviceIdType.MESH,
        )

    def rec_copy(i, step):
        return pltpu.make_async_remote_copy(
            src_ref=final[i],
            dst_ref=final_in[i].at[step],
            send_sem=rec_send.at[i, step],
            recv_sem=rec_recv.at[i, step],
            device_id={"rec": lax.rem(rec + step, recs), "frame": frame},
            device_id_type=pl.DeviceIdType.MESH,
        )

    barrier = pltpu.get_barrier_semaphore()
    pl.semaphore_signal(
        barrier,
        inc=1,
        device_id={"rec": rec, "frame": partner},
        device_id_type=pl.DeviceIdType.MESH,
    )

    @pl.loop(1, total)
    def _(step):
        j, h = place(step)
        pl.semaphore_signal(
            barrier,
            inc=1,
            device_id={"rec": h, "frame": 2 * j + core},
            device_id_type=pl.DeviceIdType.MESH,
        )

    pl.semaphore_wait(barrier, total)

    for i in range(arrays):

        @pl.loop(1, total)
        def _(step):
            pair_copy(i, step).start()

        pair_copy(i, 0).start()

    for i in range(arrays):

        @pl.loop(1, total)
        def _(step):
            j, h = place(step)
            pair_copy(i, step).wait_recv()
            pair_sum[i][j, h] = (
                ins[i][j, core, h].astype(jnp.float32) + pair_in[i][j, h].astype(jnp.float32)
            ).astype(pair_sum[i].dtype)
            chip_copy(i, step).start()

    for i in range(arrays):
        pair_copy(i, 0).wait_recv()
        own = ins[i][chip, core, rec].astype(jnp.float32) + pair_in[i][chip, rec].astype(
            jnp.float32
        )

        def add(step, value):
            chip_copy(i, step).wait_recv()
            return value + chip_in[i][step].astype(jnp.float32)

        value = lax.fori_loop(1, total, add, own).astype(final[i].dtype)
        final[i][...] = value
        for step in range(1, recs):
            rec_copy(i, step).start()
        outs[i][rec] = value.astype(jnp.float32)

    for i in range(arrays):
        for step in range(1, recs):
            rec_copy(i, step).wait_recv()
            outs[i][lax.rem(rec + recs - step, recs)] = final_in[i][step].astype(jnp.float32)

    for i in range(arrays):
        for step in range(1, recs):
            rec_copy(i, step).wait_send()
        pair_copy(i, 0).wait_send()

        @pl.loop(1, total)
        def _(step):
            pair_copy(i, step).wait_send()
            chip_copy(i, step).wait_send()


def reduce_all(parts, chips, recs):
    arrays, total = len(parts), chips * recs
    scratch = [pltpu.VMEM((chips, recs) + part.shape[3:], part.dtype) for part in parts] * 2
    scratch += [pltpu.VMEM((total,) + part.shape[3:], part.dtype) for part in parts]
    scratch += [pltpu.VMEM(part.shape[3:], part.dtype) for part in parts]
    scratch += [pltpu.VMEM((recs,) + part.shape[3:], part.dtype) for part in parts]
    scratch += [pltpu.SemaphoreType.DMA((arrays, total))] * 4
    scratch += [pltpu.SemaphoreType.DMA((arrays, recs))] * 2
    return pl.pallas_call(
        lambda *refs: reduce_kernel(chips, recs, arrays, *refs),
        name="reduce_all",
        out_shape=[jax.ShapeDtypeStruct(part.shape[2:], jnp.float32) for part in parts],
        in_specs=[pl.BlockSpec(memory_space=pltpu.VMEM)] * arrays,
        out_specs=[pl.BlockSpec(memory_space=pltpu.VMEM)] * arrays,
        scratch_shapes=scratch,
        compiler_params=pltpu.CompilerParams(
            collective_id=0, has_side_effects=True, vmem_limit_bytes=48 * 1024 * 1024
        ),
    )(*parts)


def shared_sum(grads):
    frames, recs = lax.axis_size("frame"), lax.axis_size("rec")
    split = (1, 0, 1, 0, 0, 0, 0, 0, 0, 0, 0, 0, 0)
    large = [11, 8, 6]
    rows = [grads[k].shape[0] // (frames * recs) for k in large]
    if frames % 2 or any(count == 0 or count % 16 for count in rows):
        shares = tuple(
            lax.psum_scatter(grad.astype(jnp.float32), "frame", scatter_dimension=dim, tiled=True)
            for grad, dim in zip(grads, split)
        )
        return lax.psum(shares, "rec")
    chips = frames // 2
    parts = [
        grads[k].astype(jnp.bfloat16).reshape(chips, 2, recs, count, grads[k].shape[1])
        for k, count in zip(large, rows)
    ]
    small = [k for k in range(len(grads)) if k not in large]
    pieces, shapes = [], []
    for k in small:
        grad = grads[k]
        if split[k]:
            piece = grad.reshape(grad.shape[0], frames, -1).transpose(1, 0, 2)
            shapes.append(piece.shape[1:])
            piece = piece.reshape(frames, -1)
        else:
            piece = grad.reshape(frames, -1)
            shapes.append(piece.shape[1:])
        pieces.append(piece)
    widths = [piece.shape[1] for piece in pieces]
    used = sum(widths)
    unit = 8 * 128 * recs
    padded = -(-used // unit) * unit
    packed = jnp.concatenate(pieces + [jnp.zeros((frames, padded - used), jnp.float32)], axis=1)
    parts.append(packed.reshape(chips, 2, recs, padded // (128 * recs), 128))
    sums = reduce_all(parts, chips, recs)
    out = [None] * len(grads)
    for k, total in zip(large, sums):
        out[k] = total.reshape(-1, total.shape[2])
    flat, start = sums[-1].reshape(-1), 0
    for k, width, shape in zip(small, widths, shapes):
        out[k] = flat[start : start + width].reshape(shape)
        start += width
    return tuple(out)


def body(
    code_indices,
    lengths,
    cotangent,
    embed_weight,
    embed_bias,
    depth_kernel,
    depth_bias,
    norm_gain,
    norm_bias,
    up_weight,
    up_bias,
    down_weight,
    down_bias,
    layer_scale,
    head_weight,
    head_bias,
):
    code_rows = code_indices[0]
    frame_count = code_rows.shape[0]
    total_frames = frame_count * lax.axis_size("frame")
    first_frame = lax.axis_index("frame") * frame_count
    length = lengths[0]
    frame_ids = first_frame + jnp.arange(frame_count, dtype=jnp.int32)
    valid = (frame_ids < length).astype(jnp.float32)
    values, features = embed_rows(code_rows, valid, embed_weight, embed_bias)
    rim_codes = padded_2(code_rows, (("frame", 0),), 3)
    edge_codes = jnp.concatenate([rim_codes[:3], rim_codes[frame_count + 3 :]], axis=0)
    edge_ids = jnp.concatenate(
        [
            first_frame - 3 + jnp.arange(3, dtype=jnp.int32),
            first_frame + frame_count + jnp.arange(3, dtype=jnp.int32),
        ]
    )
    edge_valid = ((edge_ids >= 0) & (edge_ids < total_frames) & (edge_ids < length)).astype(
        jnp.float32
    )
    edge_values, edge_features = embed_rows(edge_codes, edge_valid, embed_weight, embed_bias)
    padded = jnp.concatenate([edge_features[:3], features, edge_features[3:]], axis=0)
    conv_out = jnp.zeros((frame_count, features.shape[1]), jnp.float32) + depth_bias
    for tap_index in range(KERNEL):
        conv_out = conv_out + depth_kernel[tap_index] * padded[
            tap_index : tap_index + frame_count
        ].astype(jnp.float32)
    normed, norm_pullback = jax.vjp(layer_norm, conv_out, norm_gain, norm_bias)
    normed_low = normed.astype(jnp.bfloat16)
    hidden_pre = jnp.dot(normed_low, up_weight, preferred_element_type=jnp.float32) + up_bias
    activated, gelu_pullback = jax.vjp(exact_gelu, hidden_pre)
    activated_low = activated.astype(jnp.bfloat16)
    branch = jnp.dot(activated_low, down_weight, preferred_element_type=jnp.float32) + down_bias
    latent = (features.astype(jnp.float32) + layer_scale * branch).astype(jnp.bfloat16)
    logits = jnp.dot(latent, head_weight, preferred_element_type=jnp.float32) + head_bias
    spectrum, head_pullback = jax.vjp(head_map, logits)
    sample_weight = sample_scale(
        first_frame * HOP, frame_count * HOP, total_frames, HOP, NFFT, length
    )
    sample_grad = (cotangent[0].astype(jnp.float32) * sample_weight).astype(jnp.bfloat16)
    extended = padded_2(sample_grad, (("frame", 0),), PAD)
    hop_rows = extended.reshape(frame_count + 3, HOP)
    frame_grad = jnp.concatenate(
        [hop_rows[quarter : quarter + frame_count] for quarter in range(4)], axis=1
    )
    real_table, imag_table = synthesis(NFFT, BINS)
    spec_grad = jnp.concatenate(
        [
            jnp.dot(frame_grad, real_table, preferred_element_type=jnp.float32),
            jnp.dot(frame_grad, imag_table, preferred_element_type=jnp.float32),
        ],
        axis=1,
    )
    logit_grad = head_pullback(spec_grad)[0]
    logit_low = logit_grad.astype(jnp.bfloat16)
    head_weight_grad = contract_rows(latent, logit_low)
    head_bias_grad = jnp.sum(logit_grad, axis=0)
    latent_grad = contract_cols(logit_low, head_weight)
    layer_scale_grad = jnp.sum(latent_grad * branch, axis=0)
    branch_grad = layer_scale * latent_grad
    down_bias_grad = jnp.sum(branch_grad, axis=0)
    branch_low = branch_grad.astype(jnp.bfloat16)
    down_weight_grad = contract_rows(activated_low, branch_low)
    activated_grad = contract_cols(branch_low, down_weight)
    hidden_grad = gelu_pullback(activated_grad)[0]
    up_bias_grad = jnp.sum(hidden_grad, axis=0)
    hidden_low = hidden_grad.astype(jnp.bfloat16)
    up_weight_grad = contract_rows(normed_low, hidden_low)
    normed_grad = contract_cols(hidden_low, up_weight)
    conv_grad, norm_gain_grad, norm_bias_grad = norm_pullback(normed_grad)
    depth_kernel_grad = jnp.stack(
        [
            jnp.sum(
                conv_grad * padded[tap_index : tap_index + frame_count].astype(jnp.float32), axis=0
            )
            for tap_index in range(KERNEL)
        ],
        axis=0,
    )
    depth_bias_grad = jnp.sum(conv_grad, axis=0)
    conv_rims = padded_2(conv_grad.astype(jnp.bfloat16), (("frame", 0),), 3).astype(conv_grad.dtype)
    feature_grad = latent_grad
    for tap_index in range(KERNEL):
        feature_grad = (
            feature_grad
            + depth_kernel[tap_index] * conv_rims[6 - tap_index : 6 - tap_index + frame_count]
        )
    feature_grad = valid[:, None] * feature_grad
    embed_weight_grad = contract_rows(values, feature_grad, lax.Precision.HIGHEST)
    embed_bias_grad = jnp.sum(feature_grad, axis=0)
    return shared_sum(
        (
            embed_weight_grad,
            embed_bias_grad,
            depth_kernel_grad,
            depth_bias_grad,
            norm_gain_grad,
            norm_bias_grad,
            up_weight_grad,
            up_bias_grad,
            down_weight_grad,
            down_bias_grad,
            layer_scale_grad,
            head_weight_grad,
            head_bias_grad,
        )
    )


def solution(mesh):
    return jax.shard_map(
        body,
        mesh=mesh,
        in_specs=(
            P("rec", "frame", None),
            P("rec"),
            P("rec", "frame"),
            P(),
            P(),
            P(),
            P(),
            P(),
            P(),
            P(),
            P(),
            P(),
            P(),
            P(),
            P(),
            P(),
        ),
        out_specs=(
            P(None, "frame"),
            P("frame"),
            P(None, "frame"),
            P("frame"),
            P("frame"),
            P("frame"),
            P("frame", None),
            P("frame"),
            P("frame", None),
            P("frame"),
            P("frame"),
            P("frame", None),
            P("frame"),
        ),
        check_vma=False,
    )
```
